256 devices in a mesh: dp: 32 (over y_lo, z, core), tensor: 8 (over y_hi, x).
Axes of the slice: x: 4, y: 4 (y_hi: 2, y_lo: 2; y = y_hi * 2 + y_lo), z: 8, core: 2. Of those that a mesh axis runs over, the one named last changes fastest.
Arguments:
- query_states: bfloat16 [6144, 4096], P('dp', 'tensor'), may hold values from -40 to 40
- doc_states: bfloat16 [6144, 4096], P('dp', 'tensor'), may hold values from -40 to 40
- proj_weight: bfloat16 [4096, 4096], P(None, 'tensor'), may hold values from -0.09375 to 0.09375
- left_proj: bfloat16 [4096, 64], replicated, may hold values from -0.09375 to 0.09375
- right_proj: bfloat16 [4096, 64], replicated, may hold values from -5 to 5
- positives: int32 [6144], P('dp'), may hold values from 0 to 6143
Outputs:
- query_features: float32 [6144, 4096], P('dp', 'tensor')
- doc_features: float32 [6144, 4096], P('dp', 'tensor')
The draws below stay inside these ranges and needn't reach their ends.
All inputs are finite; a program needn't handle non-finite values.
Results may differ from the reference program's by a relative error of at most 0.0033.
Values may be sent and summed in bfloat16 or wider, within the bound.
No kernel may reach another device: no remote copies, remote signals or barrier semaphores. Data moves between devices by JAX's collectives and lax.ppermute only.
A program may use at most 64 MiB of HBM per device.

```python
import jax
import jax.numpy as jnp
from jax import lax

D = 4096
K1 = 64
K2 = 64
PAIR_DEV = 192
PAIRS = 6144
DSUB = 24


def draw_both(key):
    base = jax.random.fold_in(key, 4242)
    keys = jax.random.split(base, 7)
    row_ids = jnp.arange(PAIRS, dtype=jnp.int32)
    group_count = PAIR_DEV // DSUB
    group = row_ids % PAIR_DEV // DSUB
    ramp = (group.astype(jnp.float32) / jnp.float32(max(group_count - 1, 1)))[:, None]
    ramp_dir = jnp.clip(jax.random.normal(keys[6], (D,), jnp.float32), -4.0, 4.0)
    query_base = jnp.clip(jax.random.normal(keys[0], (PAIRS, D), jnp.float32), -5.0, 5.0)
    doc_base = jnp.clip(jax.random.normal(keys[1], (PAIRS, D), jnp.float32), -5.0, 5.0)
    query_base = query_base + 0.11 * ramp_dir[None, :]
    doc_base = doc_base + 0.2 * ramp * ramp_dir[None, :]
    query_scale = jnp.exp(jax.random.uniform(keys[3], (PAIRS, 1), jnp.float32, -0.7, 1.4))
    doc_scale = jnp.exp(jax.random.uniform(keys[4], (PAIRS, 1), jnp.float32, -0.7, 1.4))
    query_rows = query_base * query_scale
    doc_rows = doc_base * doc_scale
    return (jnp.clip(query_rows, -40.0, 40.0), jnp.clip(doc_rows, -40.0, 40.0))


def draw_query_states(key, part):
    return draw_both(key)[0].astype(jnp.bfloat16)


def draw_doc_states(key, part):
    return draw_both(key)[1].astype(jnp.bfloat16)


def place_ends(result, key, least, largest):
    extent = result.shape
    spot = [jax.random.randint(jax.random.fold_in(key, axis), (), 0, extent[axis]) for axis in range(len(extent))]
    result = result.at[tuple(spot)].set(least)
    longest = extent.index(max(extent))
    spot[longest] = (spot[longest] + 1) % extent[longest]
    return result.at[tuple(spot)].set(largest)


def steps_of(rng, shape, pieces, least, high):
    def one(dim, shards_of):
        draws = jax.random.uniform(jax.random.fold_in(jax.random.fold_in(rng, 6), dim), (shards_of,), jnp.float32, least / len(pieces), high / len(pieces))
        return jnp.repeat(jnp.exp(draws), shape[dim] // shards_of).reshape((-1,) + (1,) * (len(shape) - dim - 1))

    factor_of = one(*pieces[0])
    for cut in pieces[1:]:
        factor_of = factor_of * one(*cut)
    return factor_of


def normal_values(stream_key, extent, deviation, limit, cuts=(), held_as=jnp.bfloat16):
    level = steps_of(stream_key, extent, cuts, -0.22, 0.18) if cuts else 1.0
    values = jax.random.normal(stream_key, extent, jnp.float32) * deviation * level
    return jnp.minimum(jnp.maximum(values, -limit), limit).astype(held_as)


def setup_inputs(seed: int = 0) -> dict:
    seeds = jax.random.split(jax.random.key(seed), 7)
    return {
        "query_states": draw_query_states(jax.random.fold_in(seeds[6], 71), 0),
        "doc_states": draw_doc_states(jax.random.fold_in(seeds[6], 71), 0),
        "proj_weight": normal_values(seeds[2], (D, D), D ** -0.5, 0.09375, ((1, 8),)),
        "left_proj": normal_values(seeds[3], (D, K1), D ** -0.5, 0.09375),
        "right_proj": normal_values(seeds[4], (D, K2), 1.0, 5.0),
        "positives": place_ends(jax.random.randint(seeds[5], (PAIRS,), 0, PAIRS), jax.random.fold_in(seeds[5], 1), 0, PAIRS - 1).astype(jnp.int32),
    }


epsilon = 1e-06
inverse_temp = 100.0

def unit_embed(states, weight):
    raw_rows = jnp.dot(states, weight, preferred_element_type=jnp.float32)
    scale = lax.rsqrt(lax.optimization_barrier(jnp.sum(raw_rows * raw_rows, axis=1)) + epsilon)
    return ((raw_rows * scale[:, None]).astype(jnp.bfloat16), scale)

def features(states, unit, gradient, scale, left_proj, right_proj):
    unit_wide = unit.astype(jnp.float32)
    inner = lax.optimization_barrier(jnp.sum(unit_wide * gradient, axis=1))
    pulled = (gradient - unit_wide * inner[:, None]) * scale[:, None]
    right_side = jnp.dot(pulled, right_proj.astype(jnp.float32), precision=lax.Precision.HIGHEST)
    left_side = jnp.dot(states, left_proj, preferred_element_type=jnp.float32)
    return (left_side[:, :, None] * right_side[:, None, :]).reshape(states.shape[0], -1)

def reference(query_states, doc_states, proj_weight, left_proj, right_proj, positives):
    query_unit, query_scale = unit_embed(query_states, proj_weight)
    doc_unit, doc_scale = unit_embed(doc_states, proj_weight)
    scores = jnp.dot(query_unit, doc_unit.T, preferred_element_type=jnp.float32) * inverse_temp
    row_top = lax.optimization_barrier(jnp.max(scores, axis=1))
    row_sum = lax.optimization_barrier(jnp.sum(jnp.exp(scores - row_top[:, None]), axis=1))
    lse = row_top + jnp.log(row_sum)
    doc_ids = jnp.arange(PAIRS, dtype=jnp.int32)
    onehot = (positives[:, None] == doc_ids[None, :]).astype(jnp.float32)
    weights = (jnp.exp(scores - lse[:, None]) - onehot).astype(jnp.bfloat16)
    query_grad = jnp.dot(weights, doc_unit, preferred_element_type=jnp.float32) * inverse_temp
    doc_grad = jnp.dot(weights.T, query_unit, preferred_element_type=jnp.float32) * inverse_temp
    query_features = features(query_states, query_unit, query_grad, query_scale, left_proj, right_proj)
    doc_features = features(doc_states, doc_unit, doc_grad, doc_scale, left_proj, right_proj)
    return (query_features, doc_features)
```

```python
import jax
import jax.numpy as jnp
from jax import lax
from jax.sharding import Mesh
from jax.sharding import PartitionSpec as P

epsilon = 1e-06
inverse_temp = 100.0

AXES = (("ylo", 2), ("z", 8), ("core", 2), ("yhi", 2), ("x", 4))
DP = ("ylo", "z", "core")
TENSOR = ("yhi", "x")
CHIPS = ("ylo", "z")
PAIR = ("core", "yhi", "x")


def copies(array, axis):
    length = lax.axis_size(axis)
    return lax.all_to_all(
        jnp.broadcast_to(array[None], (length, *array.shape)), axis, 0, 0, tiled=True
    )


def shifted(array, axis, by):
    length = lax.axis_size(axis)
    return lax.ppermute(array, axis, [(i, (i + by) % length) for i in range(length)])


def full_width(states):
    parts = copies(states, TENSOR)
    return jnp.swapaxes(parts, 0, 1).reshape(states.shape[0], -1)


def unit_rows(raw):
    count = lax.axis_size(TENSOR)
    rows = lax.all_to_all(
        raw.reshape(count, raw.shape[0] // count, raw.shape[1]), TENSOR, 0, 0, tiled=True
    )
    scale = lax.rsqrt(jnp.sum(rows * rows, axis=(0, 2)) + epsilon)
    unit = (rows * scale[None, :, None]).astype(jnp.bfloat16)
    return jnp.swapaxes(unit, 0, 1).reshape(unit.shape[1], -1), scale


def ring_gather(block):
    half = block.shape[0] // 2
    found = [block]
    up = down = block
    for _ in range(3):
        up = shifted(up, "z", 1)
        down = shifted(down, "z", -1)
        found += [up, down]
    far = (shifted(up[:half], "z", 1), shifted(down[half:], "z", -1))
    return found + list(far)


def outer_rows(left_side, right_side):
    return (left_side[:, :, None] * right_side[:, None, :]).reshape(left_side.shape[0], -1)


def local(query_states, doc_states, proj_weight, left_proj, right_proj, positives):
    t_rank = lax.axis_index(TENSOR)
    t_count = lax.axis_size(TENSOR)
    core = lax.axis_index("core")
    ylo = lax.axis_index("ylo")
    z = lax.axis_index("z")
    rows = query_states.shape[0]
    share = rows // t_count
    left_share = left_proj.shape[1] // t_count

    doc_full = full_width(doc_states)
    doc_raw = jnp.dot(doc_full, proj_weight, preferred_element_type=jnp.float32)
    doc_mine, doc_scale = unit_rows(doc_raw)
    query_full = full_width(query_states)
    query_raw = jnp.dot(query_full, proj_weight, preferred_element_type=jnp.float32)
    query_mine, query_scale = unit_rows(query_raw)

    pair = jnp.concatenate([doc_mine, shifted(doc_mine, "ylo", 1)], axis=0)
    docs = jnp.concatenate(ring_gather(pair), axis=0)
    z_of = jnp.array([0, -1, 1, -2, 2, -3, 3, -4], dtype=jnp.int32)
    z_ids = (z + z_of + 8) % 8
    y_ids = jnp.stack([ylo, 1 - ylo])
    base = ((y_ids[None, :] * 8 + z_ids[:, None]) * 2 + core) * rows + t_rank * share
    doc_ids = (base[:, :, None] + jnp.arange(share, dtype=jnp.int32)).reshape(-1)

    query_own = copies(query_mine, TENSOR).reshape(rows, -1)
    queries = jnp.concatenate([query_own, shifted(query_own, "core", 1)], axis=0)
    wanted = jnp.concatenate([positives, shifted(positives, "core", 1)], axis=0)

    scores = (
        lax.dot_general(
            queries, docs, (((1,), (1,)), ((), ())), preferred_element_type=jnp.float32
        )
        * inverse_temp
    )
    local_top = jnp.max(scores, axis=1)
    local_sum = jnp.sum(jnp.exp(scores - local_top[:, None]), axis=1)
    stats = jnp.stack([local_top, local_sum]).reshape(2, 2, rows)
    stats = jnp.where(core == 0, stats, stats[:, ::-1])
    scale_slot = jnp.zeros((2, rows - share), jnp.float32)
    extra = jnp.concatenate([jnp.broadcast_to(query_scale, (2, share)), scale_slot], axis=1)
    everything = copies(jnp.concatenate([stats, extra[:, None, :]], axis=1), PAIR)
    tops, sums = everything[:, 0, :2], everything[:, 1, :2]
    row_top = jnp.max(tops, axis=0)
    row_sum = jnp.sum(sums * jnp.exp(tops - row_top), axis=0)
    lse = row_top + jnp.log(row_sum)
    lse = jnp.where(core == 0, lse, lse[::-1]).reshape(-1)
    scales = everything[:, 0, 2, :share].reshape(2, rows)
    scale_rows = jnp.where(core == 0, scales[0], scales[1])

    onehot = (wanted[:, None] == doc_ids[None, :]).astype(jnp.float32)
    weights = (jnp.exp(scores - lse[:, None]) - onehot).astype(jnp.bfloat16)
    wide = weights.astype(jnp.float32)
    product = wide * scores
    unit_query_proj = jnp.dot(queries, right_proj, preferred_element_type=jnp.float32)
    unit_doc_proj = jnp.dot(docs, right_proj, preferred_element_type=jnp.float32)

    doc_part = (
        lax.dot_general(
            wide, unit_query_proj, (((0,), (0,)), ((), ())), precision=lax.Precision.HIGHEST
        )
        * inverse_temp
    )
    doc_inner = jnp.sum(product, axis=0)
    doc_both = jnp.concatenate([doc_part, doc_inner[:, None]], axis=1)
    query_part = (
        jnp.dot(wide, unit_doc_proj, precision=lax.Precision.HIGHEST) * inverse_temp
    )
    query_inner = jnp.sum(product, axis=1)
    query_both = jnp.concatenate([query_part, query_inner[:, None]], axis=1)

    blocks = doc_both.reshape(8, 2, share, -1)
    place = (jnp.arange(8, dtype=jnp.int32) - z + 8) % 8
    order = jnp.array([0, 2, 4, 6, 7, 5, 3, 1], dtype=jnp.int32)
    blocks = jnp.take(blocks, jnp.take(order, place), axis=0)
    blocks = jnp.where(ylo == 0, blocks, blocks[:, ::-1])
    blocks = jnp.swapaxes(blocks, 0, 1).reshape(16, share, -1)
    doc_sum = jnp.sum(lax.all_to_all(blocks, CHIPS, 0, 0, tiled=True), axis=0)
    right_mine = (
        doc_sum[:, :-1] - doc_sum[:, -1:] * unit_doc_proj[:share]
    ) * doc_scale[:, None]
    right_doc = copies(right_mine, TENSOR).reshape(rows, -1)

    query_half = query_both[:rows] + shifted(query_both[rows:], "core", 1)
    query_sum = jnp.sum(copies(query_half, TENSOR), axis=0)
    right_query = (
        query_sum[:, :-1] - query_sum[:, -1:] * unit_query_proj[:rows]
    ) * scale_rows[:, None]

    left_mine = lax.dynamic_slice_in_dim(left_proj, t_rank * left_share, left_share, 1)
    left_query = jnp.dot(query_full, left_mine, preferred_element_type=jnp.float32)
    left_doc = jnp.dot(doc_full, left_mine, preferred_element_type=jnp.float32)
    return outer_rows(left_query, right_query), outer_rows(left_doc, right_doc)


def solution(mesh):
    names = tuple(name for name, _ in AXES)
    finer = Mesh(mesh.devices.reshape([size for _, size in AXES]), names)
    placed = (P(DP, TENSOR), P(DP, TENSOR), P(None, TENSOR), P(), P(), P(DP))
    return jax.shard_map(
        local,
        mesh=finer,
        in_specs=placed,
        out_specs=(P(DP, TENSOR), P(DP, TENSOR)),
        check_vma=False,
    )
```

```python
import jax
import jax.numpy as jnp
from jax import lax
from jax.experimental import pallas as pl
from jax.experimental.pallas import tpu as pltpu
from jax.sharding import Mesh
from jax.sharding import PartitionSpec as P

epsilon = 1e-06
inverse_temp = 100.0

AXES = (("ylo", 2), ("z", 8), ("core", 2), ("yhi", 2), ("x", 4))
DP = ("ylo", "z", "core")
TENSOR = ("yhi", "x")
CHIPS = ("ylo", "z")
PAIR = ("core", "yhi", "x")


def copies(array, axis):
    length = lax.axis_size(axis)
    return lax.all_to_all(
        jnp.broadcast_to(array[None], (length, *array.shape)), axis, 0, 0, tiled=True
    )


def shifted(array, axis, by):
    length = lax.axis_size(axis)
    return lax.ppermute(array, axis, [(i, (i + by) % length) for i in range(length)])


def raw_kernel(yhi_ref, doc_ref, near_ref, far_ref, weight_ref, out_ref, doc_acc, query_acc):
    step = pl.program_id(0)
    weight = weight_ref[...]
    doc = jnp.dot(doc_ref[0, 0], weight, preferred_element_type=jnp.float32)
    states = jnp.where(step < 4, near_ref[0], far_ref[0])
    query = jnp.dot(states, weight, preferred_element_type=jnp.float32)

    @pl.when(step == 0)
    def _():
        doc_acc[...] = doc
        query_acc[...] = query

    @pl.when(step > 0)
    def _():
        doc_acc[...] += doc
        query_acc[...] += query

    @pl.when(step == pl.num_programs(0) - 1)
    def _():
        count, both = out_ref.shape[0], out_ref.shape[1]
        for k in range(count):
            rows = pl.ds(k * (both // 2), both // 2)
            out_ref[k, : both // 2] = doc_acc[rows]
            out_ref[k, both // 2 :] = query_acc[rows]


def raw_rows(docs, near, far, weight, yhi):
    _, _, rows, width = docs.shape
    cols = weight.shape[1]
    share = rows // 8
    grid = pltpu.PrefetchScalarGridSpec(
        num_scalar_prefetch=1,
        grid=(8,),
        in_specs=[
            pl.BlockSpec((1, 1, rows, width), lambda k, y: (k % 4, k // 4, 0, 0)),
            pl.BlockSpec((1, rows, width), lambda k, y: (jnp.minimum(k, 3), 0, 0)),
            pl.BlockSpec((1, rows, width), lambda k, y: (jnp.maximum(k - 4, 0), 0, 0)),
            pl.BlockSpec((width, cols), lambda k, y: ((y[0] + k // 4) % 2 * 4 + k % 4, 0)),
        ],
        out_specs=pl.BlockSpec((8, 2 * share, cols), lambda k, y: (0, 0, 0)),
        scratch_shapes=[pltpu.VMEM((rows, cols), jnp.float32)] * 2,
    )
    return pl.pallas_call(
        raw_kernel,
        grid_spec=grid,
        out_shape=jax.ShapeDtypeStruct((8, 2 * share, cols), jnp.float32),
        name="raw_rows",
    )(yhi.reshape(1), docs, near, far, weight)


def unit_kernel(raw_ref, doc_ref, query_ref, scale_ref):
    count, both, width = raw_ref.shape
    total = jnp.zeros((both, 1), jnp.float32)
    for k in range(count):
        part = raw_ref[k]
        total += jnp.sum(part * part, axis=1, keepdims=True)
    scale = lax.rsqrt(total + epsilon)
    scale_ref[...] = scale
    for k in range(count):
        unit = (raw_ref[k] * scale).astype(jnp.bfloat16)
        cols = pl.ds(k * width, width)
        doc_ref[:, cols] = unit[: both // 2]
        query_ref[:, cols] = unit[both // 2 :]


def unit_rows(raw):
    count, both, width = raw.shape
    rows = jax.ShapeDtypeStruct((both // 2, count * width), jnp.bfloat16)
    return pl.pallas_call(
        unit_kernel,
        out_shape=(rows, rows, jax.ShapeDtypeStruct((both, 1), jnp.float32)),
        name="unit_rows",
    )(raw)


def ring_gather(near, far):
    found = [near, far]
    near_up = near_down = near
    far_up = far_down = far
    for _ in range(3):
        near_up, near_down = shifted(near_up, "z", 1), shifted(near_down, "z", -1)
        far_up, far_down = shifted(far_up, "z", 1), shifted(far_down, "z", -1)
        found += [near_up, far_up, near_down, far_down]
    return found + [shifted(near_up, "z", 1), shifted(far_down, "z", -1)]


def outer_rows(left_side, right_side):
    return (left_side[:, :, None] * right_side[:, None, :]).reshape(left_side.shape[0], -1)


def local(query_states, doc_states, proj_weight, left_proj, right_proj, positives):
    t_rank = lax.axis_index(TENSOR)
    t_count = lax.axis_size(TENSOR)
    core = lax.axis_index("core")
    ylo = lax.axis_index("ylo")
    z = lax.axis_index("z")
    rows = query_states.shape[0]
    share = rows // t_count
    left_share = left_proj.shape[1] // t_count

    yhi = lax.axis_index("yhi")
    doc_far = shifted(doc_states, "yhi", 1)
    query_near = copies(query_states, "x")
    query_far = shifted(query_near, "yhi", 1)
    doc_full = copies(jnp.stack([doc_states, doc_far]), "x")
    raw = raw_rows(doc_full, query_near, query_far, proj_weight, yhi)
    raw = lax.all_to_all(raw, TENSOR, 0, 0, tiled=True)
    doc_mine, query_mine, scale_mine = unit_rows(raw)
    doc_scale, query_scale = scale_mine[:share, 0], scale_mine[share:, 0]

    docs = jnp.concatenate(ring_gather(doc_mine, shifted(doc_mine, "ylo", 1)), axis=0)
    z_of = jnp.array([0, -1, 1, -2, 2, -3, 3, -4], dtype=jnp.int32)
    z_ids = (z + z_of + 8) % 8
    y_ids = jnp.stack([ylo, 1 - ylo])
    base = ((y_ids[None, :] * 8 + z_ids[:, None]) * 2 + core) * rows + t_rank * share
    doc_ids = (base[:, :, None] + jnp.arange(share, dtype=jnp.int32)).reshape(-1)

    query_own = copies(query_mine, TENSOR).reshape(rows, -1)
    queries = jnp.concatenate([query_own, shifted(query_own, "core", 1)], axis=0)
    wanted = jnp.concatenate([positives, shifted(positives, "core", 1)], axis=0)

    scores = (
        lax.dot_general(
            queries, docs, (((1,), (1,)), ((), ())), preferred_element_type=jnp.float32
        )
        * inverse_temp
    )
    local_top = jnp.max(scores, axis=1)
    local_sum = jnp.sum(jnp.exp(scores - local_top[:, None]), axis=1)
    stats = jnp.stack([local_top, local_sum]).reshape(2, 2, rows)
    stats = jnp.where(core == 0, stats, stats[:, ::-1])
    scale_slot = jnp.zeros((2, rows - share), jnp.float32)
    extra = jnp.concatenate([jnp.broadcast_to(query_scale, (2, share)), scale_slot], axis=1)
    everything = copies(jnp.concatenate([stats, extra[:, None, :]], axis=1), PAIR)
    tops, sums = everything[:, 0, :2], everything[:, 1, :2]
    row_top = jnp.max(tops, axis=0)
    row_sum = jnp.sum(sums * jnp.exp(tops - row_top), axis=0)
    lse = row_top + jnp.log(row_sum)
    lse = jnp.where(core == 0, lse, lse[::-1]).reshape(-1)
    scales = everything[:, 0, 2, :share].reshape(2, rows)
    scale_rows = jnp.where(core == 0, scales[0], scales[1])

    onehot = (wanted[:, None] == doc_ids[None, :]).astype(jnp.float32)
    weights = (jnp.exp(scores - lse[:, None]) - onehot).astype(jnp.bfloat16)
    wide = weights.astype(jnp.float32)
    product = wide * scores
    unit_query_proj = jnp.dot(queries, right_proj, preferred_element_type=jnp.float32)
    unit_doc_proj = jnp.dot(docs, right_proj, preferred_element_type=jnp.float32)

    doc_part = (
        lax.dot_general(
            wide, unit_query_proj, (((0,), (0,)), ((), ())), precision=lax.Precision.HIGHEST
        )
        * inverse_temp
    )
    doc_inner = jnp.sum(product, axis=0)
    doc_both = jnp.concatenate([doc_part, doc_inner[:, None]], axis=1)
    query_part = (
        jnp.dot(wide, unit_doc_proj, precision=lax.Precision.HIGHEST) * inverse_temp
    )
    query_inner = jnp.sum(product, axis=1)
    query_both = jnp.concatenate([query_part, query_inner[:, None]], axis=1)

    blocks = doc_both.reshape(8, 2, share, -1)
    place = (jnp.arange(8, dtype=jnp.int32) - z + 8) % 8
    order = jnp.array([0, 2, 4, 6, 7, 5, 3, 1], dtype=jnp.int32)
    blocks = jnp.take(blocks, jnp.take(order, place), axis=0)
    blocks = jnp.where(ylo == 0, blocks, blocks[:, ::-1])
    blocks = jnp.swapaxes(blocks, 0, 1).reshape(16, share, -1)
    doc_sum = jnp.sum(lax.all_to_all(blocks, CHIPS, 0, 0, tiled=True), axis=0)
    right_mine = (
        doc_sum[:, :-1] - doc_sum[:, -1:] * unit_doc_proj[:share]
    ) * doc_scale[:, None]
    query_half = query_both[:rows] + shifted(query_both[rows:], "core", 1)
    last = jnp.pad(right_mine, ((0, 0), (0, 1)))
    arrived = copies(jnp.concatenate([query_half, last], axis=0), TENSOR)
    right_doc = arrived[:, rows:, :-1].reshape(rows, -1)
    query_sum = jnp.sum(arrived[:, :rows], axis=0)
    right_query = (
        query_sum[:, :-1] - query_sum[:, -1:] * unit_query_proj[:rows]
    ) * scale_rows[:, None]

    left_mine = lax.dynamic_slice_in_dim(left_proj, t_rank * left_share, left_share, 1)
    left_parts = left_mine.reshape(2, 4, -1, left_share)
    left_parts = jnp.where(yhi == 0, left_parts, left_parts[::-1])
    left_query = sum(
        jnp.dot(part[k], left_parts[side, k], preferred_element_type=jnp.float32)
        for side, part in enumerate((query_near, query_far))
        for k in range(4)
    )
    left_doc = sum(
        jnp.dot(doc_full[k, side], left_parts[side, k], preferred_element_type=jnp.float32)
        for side in range(2)
        for k in range(4)
    )
    return outer_rows(left_query, right_query), outer_rows(left_doc, right_doc)


def solution(mesh):
    names = tuple(name for name, _ in AXES)
    finer = Mesh(mesh.devices.reshape([size for _, size in AXES]), names)
    placed = (P(DP, TENSOR), P(DP, TENSOR), P(None, TENSOR), P(), P(), P(DP))
    return jax.shard_map(
        local,
        mesh=finer,
        in_specs=placed,
        out_specs=(P(DP, TENSOR), P(DP, TENSOR)),
        check_vma=False,
    )
```

```python
import jax
import jax.numpy as jnp
from jax import lax
from jax.experimental import pallas as pl
from jax.experimental.pallas import tpu as pltpu
from jax.sharding import Mesh
from jax.sharding import PartitionSpec as P

epsilon = 1e-06
inverse_temp = 100.0

AXES = (("ylo", 2), ("z", 8), ("core", 2), ("yhi", 2), ("x", 4))
DP = ("ylo", "z", "core")
TENSOR = ("yhi", "x")
CHIPS = ("ylo", "z")
PAIR = ("core", "yhi", "x")


def copies(array, axis):
    length = lax.axis_size(axis)
    return lax.all_to_all(
        jnp.broadcast_to(array[None], (length, *array.shape)), axis, 0, 0, tiled=True
    )


def shifted(array, axis, by):
    length = lax.axis_size(axis)
    return lax.ppermute(array, axis, [(i, (i + by) % length) for i in range(length)])


def raw_kernel(yhi_ref, doc_ref, near_ref, far_ref, left_ref, weight_ref, *refs):
    doc_out, query_out, doc_left, query_left, weights, done = refs
    rows, width = near_ref.shape[1:]
    yhi = yhi_ref[0]

    def block(k):
        return (yhi + k // 4) % 2 * 4 + k % 4

    def fetch(k):
        at = pl.multiple_of(block(k) * width, width)
        return pltpu.make_async_copy(
            weight_ref.at[pl.ds(at, width)], weights.at[pl.ds(k * width, width)], done.at[k]
        )

    for k in range(8):
        fetch(k).start()

    def states(docs, side):
        if docs:
            parts = [doc_ref[k, side] for k in range(4)]
        else:
            parts = [(near_ref, far_ref)[side][k] for k in range(4)]
        return jnp.concatenate(parts, axis=1)

    for docs, out in ((True, doc_left), (False, query_left)):
        total = 0.0
        for side in range(2):
            part = states(docs, side)
            left = jnp.concatenate([left_ref[block(side * 4 + k)] for k in range(4)], axis=1)
            total += lax.dot_general(
                part, left, (((1,), (1,)), ((), ())), preferred_element_type=jnp.float32
            )
        out[...] = total

    doc = query = 0.0
    for side in range(2):
        for k in range(4):
            fetch(side * 4 + k).wait()
        weight = weights[pl.ds(side * 4 * width, 4 * width)]
        doc += jnp.dot(states(True, side), weight, preferred_element_type=jnp.float32)
        query += jnp.dot(states(False, side), weight, preferred_element_type=jnp.float32)

    share = rows // 8
    doc_out[:, :share] = doc.reshape(8, share, -1)
    squares = lax.dot_general(
        jnp.ones((8, query.shape[1]), jnp.float32),
        query * query,
        (((1,), (1,)), ((), ())),
        precision=lax.Precision.HIGHEST,
        preferred_element_type=jnp.float32,
    )
    for k in range(8):
        doc_out[k, share:] = jnp.zeros((8, doc_out.shape[2]), jnp.float32)
        doc_out[k, share:, :rows] = squares
    query_out[...] = query


def raw_rows(docs, near, far, weight, left, yhi):
    rows, cols = docs.shape[2], weight.shape[1]
    there = [pltpu.with_memory_space_constraint(a, pltpu.VMEM) for a in (docs, near, far)]
    vmem = pl.BlockSpec(memory_space=pltpu.VMEM)
    return pl.pallas_call(
        raw_kernel,
        in_specs=[pl.BlockSpec(memory_space=pltpu.SMEM), vmem, vmem, vmem, vmem]
        + [pl.BlockSpec(memory_space=pltpu.HBM)],
        out_shape=(
            jax.ShapeDtypeStruct((8, rows // 8 + 8, cols), jnp.float32),
            jax.ShapeDtypeStruct((rows, cols), jnp.float32),
            jax.ShapeDtypeStruct((rows, left.shape[1]), jnp.float32),
            jax.ShapeDtypeStruct((rows, left.shape[1]), jnp.float32),
        ),
        scratch_shapes=[
            pltpu.VMEM(weight.shape, weight.dtype),
            pltpu.SemaphoreType.DMA((8,)),
        ],
        name="raw_rows",
        compiler_params=pltpu.CompilerParams(vmem_limit_bytes=20 << 20),
    )(yhi.reshape(1), *there, left, pltpu.with_memory_space_constraint(weight, pltpu.HBM))


def unit_kernel(raw_ref, query_ref, doc_out, query_out, doc_scale, query_scale):
    count, both, width = raw_ref.shape
    share, rows = both - 8, query_ref.shape[0]
    total = jnp.zeros((share, 1), jnp.float32)
    squares = jnp.zeros((8, 256), jnp.float32)
    for k in range(count):
        part = raw_ref[k, :share]
        total += jnp.sum(part * part, axis=1, keepdims=True)
        squares += raw_ref[k, share:, :256]
    scale = lax.rsqrt(total + epsilon)
    doc_scale[...] = scale
    for k in range(count):
        doc_out[:, pl.ds(k * width, width)] = (raw_ref[k, :share] * scale).astype(jnp.bfloat16)
    scale = lax.rsqrt(squares.T[:rows, :1] + epsilon)
    query_scale[...] = scale
    query_out[...] = (query_ref[...] * scale).astype(jnp.bfloat16)


def unit_rows(raw, query):
    count, both, width = raw.shape
    rows = query.shape[0]
    return pl.pallas_call(
        unit_kernel,
        out_shape=(
            jax.ShapeDtypeStruct((both - 8, count * width), jnp.bfloat16),
            jax.ShapeDtypeStruct((rows, width), jnp.bfloat16),
            jax.ShapeDtypeStruct((both - 8, 1), jnp.float32),
            jax.ShapeDtypeStruct((rows, 1), jnp.float32),
        ),
        name="unit_rows",
        compiler_params=pltpu.CompilerParams(vmem_limit_bytes=16 << 20),
    )(raw, query)


def ring_gather(near, far):
    found = [near, far]
    near_up = near_down = near
    far_up = far_down = far
    for _ in range(1, 4):
        near_up = shifted(near_up, "z", 1)
        near_down = shifted(near_down, "z", -1)
        far_up = shifted(far_up, "z", 1)
        far_down = shifted(far_down, "z", -1)
        found += [near_up, far_up, near_down, far_down]
    near_up = shifted(near_up, "z", 1)
    far_down = shifted(far_down, "z", -1)
    return found + [near_up, far_down]


def outer_rows(left_side, right_side):
    return (left_side[:, :, None] * right_side[:, None, :]).reshape(left_side.shape[0], -1)


def local(query_states, doc_states, proj_weight, left_proj, right_proj, positives):
    t_rank = lax.axis_index(TENSOR)
    t_count = lax.axis_size(TENSOR)
    core = lax.axis_index("core")
    ylo = lax.axis_index("ylo")
    yhi = lax.axis_index("yhi")
    z = lax.axis_index("z")
    rows = query_states.shape[0]
    share = rows // t_count
    left_share = left_proj.shape[1] // t_count

    left_mine = lax.dynamic_slice_in_dim(left_proj.T, t_rank * left_share, left_share, 0)
    left_mine = jnp.swapaxes(left_mine.reshape(left_share, t_count, -1), 0, 1)

    doc_far = shifted(doc_states, "yhi", 1)
    query_near = copies(query_states, "x")
    query_far = shifted(query_near, "yhi", 1)
    doc_full = copies(jnp.stack([doc_states, doc_far]), "x")
    raw, query_raw, left_doc, left_query = raw_rows(
        doc_full, query_near, query_far, proj_weight, left_mine, yhi
    )
    raw = lax.all_to_all(raw, TENSOR, 0, 0, tiled=True)
    doc_mine, query_mine, doc_scale, query_scale = unit_rows(raw, query_raw)

    blocks = ring_gather(doc_mine, shifted(doc_mine, "ylo", 1))
    docs = jnp.concatenate(blocks, axis=0)
    z_of = jnp.array([0, -1, 1, -2, 2, -3, 3, -4], dtype=jnp.int32)
    z_ids = (z + z_of + 8) % 8
    y_ids = jnp.stack([ylo, 1 - ylo])
    base = ((y_ids[None, :] * 8 + z_ids[:, None]) * 2 + core) * rows + t_rank * share
    doc_ids = (base[:, :, None] + jnp.arange(share, dtype=jnp.int32)).reshape(-1)

    query_own = copies(query_mine, TENSOR)
    query_own, _ = lax.optimization_barrier((query_own, blocks[10:14]))
    query_own = jnp.swapaxes(query_own, 0, 1).reshape(rows, -1)
    query_other = shifted(query_own, "core", 1)
    queries = jnp.concatenate([query_own, query_other], axis=0)
    wanted = jnp.concatenate([positives, shifted(positives, "core", 1)], axis=0)

    scores = (
        lax.dot_general(
            queries, docs, (((1,), (1,)), ((), ())), preferred_element_type=jnp.float32
        )
        * inverse_temp
    )
    local_top = jnp.max(scores, axis=1)
    local_sum = jnp.sum(jnp.exp(scores - local_top[:, None]), axis=1)
    stats = jnp.stack([local_top, local_sum]).reshape(2, 2, rows)
    stats = jnp.where(core == 0, stats, stats[:, ::-1])
    everything = copies(stats, PAIR)
    tops, sums = everything[:, 0], everything[:, 1]
    row_top = jnp.max(tops, axis=0)
    row_sum = jnp.sum(sums * jnp.exp(tops - row_top), axis=0)
    lse = row_top + jnp.log(row_sum)
    lse = jnp.where(core == 0, lse, lse[::-1]).reshape(-1)

    onehot = (wanted[:, None] == doc_ids[None, :]).astype(jnp.float32)
    weights = (jnp.exp(scores - lse[:, None]) - onehot).astype(jnp.bfloat16)
    wide = weights.astype(jnp.float32)
    product = wide * scores
    unit_query_proj = jnp.dot(queries, right_proj, preferred_element_type=jnp.float32)
    unit_doc_proj = jnp.dot(docs, right_proj, preferred_element_type=jnp.float32)

    doc_part = (
        lax.dot_general(
            wide, unit_query_proj, (((0,), (0,)), ((), ())), precision=lax.Precision.HIGHEST
        )
        * inverse_temp
        - jnp.sum(product, axis=0)[:, None] * unit_doc_proj
    )
    query_part = (
        jnp.dot(wide, unit_doc_proj, precision=lax.Precision.HIGHEST) * inverse_temp
        - jnp.sum(product, axis=1)[:, None] * unit_query_proj
    )

    part = doc_part.reshape(8, 2, share, -1)
    place = (jnp.arange(8, dtype=jnp.int32) - z + 8) % 8
    order = jnp.array([0, 2, 4, 6, 7, 5, 3, 1], dtype=jnp.int32)
    part = jnp.take(part, jnp.take(order, place), axis=0)
    part = jnp.where(ylo == 0, part, part[:, ::-1])
    part = jnp.swapaxes(part, 0, 1).reshape(16, share, -1)
    right_mine = jnp.sum(lax.all_to_all(part, CHIPS, 0, 0, tiled=True), axis=0) * doc_scale

    query_half = query_part[:rows] + shifted(query_part[rows:], "core", 1)
    arrived = copies(jnp.concatenate([query_half, right_mine], axis=0), TENSOR)
    right_doc = arrived[:, rows:].reshape(rows, -1)
    right_query = jnp.sum(arrived[:, :rows], axis=0) * query_scale
    return outer_rows(left_query, right_query), outer_rows(left_doc, right_doc)


def solution(mesh):
    names = tuple(name for name, _ in AXES)
    finer = Mesh(mesh.devices.reshape([size for _, size in AXES]), names)
    placed = (P(DP, TENSOR), P(DP, TENSOR), P(None, TENSOR), P(), P(), P(DP))
    return jax.shard_map(
        local,
        mesh=finer,
        in_specs=placed,
        out_specs=(P(DP, TENSOR), P(DP, TENSOR)),
        check_vma=False,
    )
```
